256 devices in a mesh: section: 4 (over y_hi, core), dp: 64 (over x, y_lo, z).
Axes of the slice: x: 4, y: 4 (y_hi: 2, y_lo: 2; y = y_hi * 2 + y_lo), z: 8, core: 2. Of those that a mesh axis runs over, the one named last changes fastest.
Arguments:
- activations: bfloat16 [4, 16384, 8192], P('section', 'dp'), may hold values from -600 to 600, as said below
- tail_grads: bfloat16 [4, 16384, 512], P('section', 'dp'), may hold values from -48 to 48, as said below
- tail_slots: int32 [4, 64, 4], P('section', 'dp'), may hold values from 0 to 3, each once within a row
- master: float32 [4, 8192, 512], P('section', 'dp'), may hold values from -6 to 6
- moment1: float32 [4, 8192, 512], P('section', 'dp'), may hold values from -0.00029296876 to 0.00029296876
- moment2: float32 [4, 8192, 512], P('section', 'dp'), may hold values from 1.1920929e-09 to 2.9802322e-08
- overflow: int32 [4, 64], P('section', 'dp'), may hold values from 0 to 1, as said below
- clip_on: int32 [4], P('section'), may hold values from 0 to 1, as said below
- next_inputs: bfloat16 [4, 2048, 8192], P('section', 'dp'), may hold values from -6 to 6
Outputs:
- new_master: float32 [4, 8192, 512], P('section', 'dp')
- next_out: bfloat16 [4, 2048, 512], P('section', 'dp')
The draws below stay inside these ranges and needn't reach their ends.
Inputs may be any that keep to these rules, and one draw needn't show every extreme that they name: `tail_slots`: each row along the last dimension names every slot once. `overflow`: at least one shard is flagged and at least one is not. `clip_on`: at least one section is clipped and at least one is not. `activations`: real-valued. `tail_grads`: real-valued.
All inputs are finite; a program needn't handle non-finite values.
Results may differ from the reference program's by a relative error of at most 0.0049.
Values may be sent and summed in bfloat16 or wider, within the bound.
No kernel may reach another device: no remote copies, remote signals or barrier semaphores. Data moves between devices by JAX's collectives and lax.ppermute only.
A program may use at most 64 MiB of HBM per device.

```python
import math
import jax
import jax.numpy as jnp
from jax import lax

D = 8192
TAILS = 4
TAIL_TOK = 64
COLS = 512
TOK_DEV = 256
TOKENS = 16384
NEXT_ALL = 2048
N_SECTION = 4
N_DP = 64


def draw_activations(key, part):
    keys = jax.random.split(jax.random.fold_in(key, 11), 3)
    shape = (N_SECTION, TOKENS, D)
    position = jnp.arange(D, dtype=jnp.float32) / D
    rough = jax.random.uniform(keys[1], (N_SECTION, 1, D), jnp.float32, 0.6, 1.4)
    base = jax.random.truncated_normal(keys[0], -4.0, 4.0, shape, jnp.float32)
    column = 10.0 ** position * rough
    section_scale = 1.0 + 2.0 * jnp.arange(N_SECTION, dtype=jnp.float32) / max(N_SECTION - 1, 1)

    def pairing_of(sub):
        return jax.random.permutation(sub, N_DP)
    pairing = jax.vmap(pairing_of)(jax.random.split(keys[2], N_SECTION))
    row_owner = jnp.arange(TOKENS, dtype=jnp.int32) // TOK_DEV
    col_block = jnp.arange(D, dtype=jnp.int32) // (D // N_DP)
    matched = pairing[:, row_owner]
    spike = jnp.where(matched[:, :, None] == col_block[None, None, :], 3.0, 1.0)
    return (base * column * section_scale[:, None, None] * spike).astype(jnp.bfloat16)


def draw_tail_grads(key, part):
    keys = jax.random.split(jax.random.fold_in(key, 23), 2)
    shape = (N_SECTION, TOKENS, COLS)
    spread = jax.random.uniform(keys[1], (N_SECTION, 1, COLS), jnp.float32, 0.0, 1.0)
    base = jax.random.truncated_normal(keys[0], -4.0, 4.0, shape, jnp.float32)
    column = 10.0 ** spread
    return (base * column).astype(jnp.bfloat16)


def section_marks(key, salt, lowest, highest):
    keys = jax.random.split(jax.random.fold_in(key, salt), 2)
    count = jax.random.randint(keys[0], (), lowest, highest + 1, dtype=jnp.int32)
    order = jax.random.permutation(keys[1], N_SECTION).astype(jnp.int32)
    return (order < count).astype(jnp.int32)


def draw_overflow(key, part):
    keys = jax.random.split(jax.random.fold_in(key, 53), 2)
    total = N_SECTION * N_DP
    marks = (jax.random.randint(keys[0], (total,), 0, 4, dtype=jnp.int32) == 0).astype(jnp.int32)
    order = jax.random.permutation(keys[1], total).astype(jnp.int32)
    marks = marks.at[order[0]].set(1)
    marks = marks.at[order[1]].set(0)
    return marks.reshape(N_SECTION, N_DP)


def draw_clip_on(key, part):
    return section_marks(key, 41, 1, max(N_SECTION - 1, 1))


def shard_levels(stream_key, extent, pieces, least, high):
    def one(dim, parts):
        draws = jax.random.uniform(jax.random.fold_in(jax.random.fold_in(stream_key, 6), dim), (parts,), jnp.float32, least / len(pieces), high / len(pieces))
        return jnp.repeat(jnp.exp(draws), extent[dim] // parts).reshape((-1,) + (1,) * (len(extent) - dim - 1))

    level = one(*pieces[0])
    for cut in pieces[1:]:
        level = level * one(*cut)
    return level


def noise(key, extent, deviation, limit, cuts=(), kind=jnp.bfloat16):
    entries = jax.random.normal(key, extent, jnp.float32) * deviation
    if len(cuts) > 0:
        entries = shard_levels(key, extent, cuts, -0.22, 0.18) * entries
    return jnp.clip(entries, min=-limit, max=limit).astype(kind)


def setup_inputs(seed: int = 0) -> dict:
    key_of = jax.random.split(jax.random.key(seed), 10)
    activations = draw_activations(jax.random.fold_in(key_of[9], 71), 0)
    tail_grads = draw_tail_grads(jax.random.fold_in(key_of[9], 71), 0)
    tail_slots = jax.vmap(lambda own: jax.random.permutation(own, TAILS))(jax.random.split(key_of[2], N_SECTION * N_DP)).reshape((N_SECTION, N_DP, TAILS)).astype(jnp.int32)
    master = noise(key_of[3], (N_SECTION, D, COLS), 1.0, 6.0, ((0, 4), (1, 64)), jnp.float32)
    moment1 = noise(key_of[4], (N_SECTION, D, COLS), (0.2 / (N_SECTION * D * COLS) ** 0.5), 0.00029296876, ((0, 4), (1, 64)), jnp.float32)
    moment2 = jnp.clip(jnp.exp(math.log(2.9802322387695312e-08) - 3.218876 * jax.random.uniform(key_of[5], (N_SECTION, D, COLS), jnp.float32) ** shard_levels(key_of[5], (N_SECTION, D, COLS), ((0, 4), (1, 64)), -0.2, 0.2)), 1.19209286886246e-09, 2.9802322387695312e-08)
    overflow = draw_overflow(jax.random.fold_in(key_of[9], 71), 0)
    clip_on = draw_clip_on(jax.random.fold_in(key_of[9], 71), 0)
    next_inputs = noise(key_of[8], (N_SECTION, NEXT_ALL, D), 1.0, 6.0, ((0, 4), (1, 64)))
    return dict(activations=activations, tail_grads=tail_grads, tail_slots=tail_slots, master=master, moment1=moment1, moment2=moment2, overflow=overflow, clip_on=clip_on, next_inputs=next_inputs)


beta_one = 0.9
beta_two = 0.95
correct_one = 1.0 - 0.9 ** 20
correct_two = 1.0 - 0.95 ** 20
adam_eps = 1e-08
decay_rate = 0.1
learn_rate = 0.1

def section_gradient(operands):
    stashed, tails, slots = operands
    onehot = (slots[:, :, None] == jnp.arange(TAILS, dtype=jnp.int32)[None, None, :]).astype(jnp.float32)
    shaped = tails.reshape(N_DP, TAILS, TAIL_TOK, COLS).astype(jnp.float32)
    paired = jnp.einsum('etk,etnc->eknc', onehot, shaped).astype(jnp.bfloat16).reshape(TOKENS, COLS)
    summed = lax.dot_general(stashed, paired, (((0,), (0,)), ((), ())), preferred_element_type=jnp.float32)
    return summed * (1.0 / TOKENS)

def section_forward(operands):
    inputs, weights = operands
    return jnp.dot(inputs, weights, preferred_element_type=jnp.float32)

def reference(activations, tail_grads, tail_slots, master, moment1, moment2, overflow, clip_on, next_inputs):
    grads = lax.map(section_gradient, (activations, tail_grads, tail_slots))
    keep_shard = (overflow == 0).astype(jnp.float32)
    keep = jnp.repeat(keep_shard, D // N_DP, axis=1)
    sumsq = jnp.sum(keep[:, :, None] * (grads * grads))
    norm_value = jnp.sqrt(sumsq)
    factor = jnp.where(clip_on == 1, 1.0 / jnp.maximum(norm_value, 1.0), 1.0).astype(jnp.float32)
    clipped = grads * factor[:, None, None]
    m_next = beta_one * moment1 + (1.0 - beta_one) * clipped
    v_next = beta_two * moment2 + (1.0 - beta_two) * (clipped * clipped)
    update = m_next / correct_one / (jnp.sqrt(v_next / correct_two) + adam_eps) + decay_rate * master
    new_master = jnp.where(keep[:, :, None] > 0.5, master - learn_rate * update, master)
    weights = new_master.astype(jnp.bfloat16)
    result = lax.map(section_forward, (next_inputs, weights))
    next_out = (result * (1.0 / math.sqrt(D))).astype(jnp.bfloat16)
    return (new_master, next_out)
```

```python
import math

import jax
import jax.numpy as jnp
from jax import lax
from jax.experimental import pallas as pl
from jax.experimental.pallas import tpu as pltpu
from jax.sharding import Mesh
from jax.sharding import PartitionSpec as P

DP = ("x", "y_lo", "z")
XZ = ("x", "z")
YZ = ("y_lo", "z")
SECTION = ("y_hi", "core")
EVERY = SECTION + DP

NX, NY, NZ = 4, 2, 8

beta_one = 0.9
beta_two = 0.95
correct_one = 1.0 - 0.9**20
correct_two = 1.0 - 0.95**20
adam_eps = 1e-08
decay_rate = 0.1
learn_rate = 0.1


def gradient_kernel(slots_ref, tails_ref, acts_ref, out_ref, paired_ref):
    tail = tails_ref.shape[0] // slots_ref.shape[0]

    @pl.when((pl.program_id(0) == 0) & (pl.program_id(1) == 0))
    def _():
        def place(t, carry):
            src = pl.ds(pl.multiple_of(t * tail, tail), tail)
            dst = pl.ds(pl.multiple_of(slots_ref[t] * tail, tail), tail)
            paired_ref[dst, :] = tails_ref[src, :]
            return carry

        lax.fori_loop(0, slots_ref.shape[0], place, 0)

    product = lax.dot_general(
        paired_ref[...],
        acts_ref[...],
        (((0,), (0,)), ((), ())),
        preferred_element_type=jnp.float32,
    ).astype(out_ref.dtype)
    rows = out_ref.shape[-1]
    for k in range(out_ref.shape[1]):
        out_ref[0, k, 0] = product[:, k * rows : (k + 1) * rows]


def gradient_terms(slots, tails, acts):
    tokens, width = acts.shape
    cols = tails.shape[1]
    rows = width // (NX * NY * NZ)
    return pl.pallas_call(
        gradient_kernel,
        grid_spec=pltpu.PrefetchScalarGridSpec(
            num_scalar_prefetch=1,
            grid=(NX, NY),
            in_specs=[
                pl.BlockSpec((tokens, cols), lambda i, j, s: (0, 0)),
                pl.BlockSpec((tokens, NZ * rows), lambda i, j, s: (0, i * NY + j)),
            ],
            out_specs=pl.BlockSpec((1, NZ, 1, cols, rows), lambda i, j, s: (i, 0, j, 0, 0)),
            scratch_shapes=[pltpu.VMEM((tokens, cols), tails.dtype)],
        ),
        out_shape=jax.ShapeDtypeStruct((NX, NZ, NY, cols, rows), jnp.bfloat16),
        name="gradient_terms",
    )(slots, tails, acts)


def swap_pair(x):
    return lax.ppermute(x, "y_lo", [(0, 1), (1, 0)])


def local(
    activations, tail_grads, tail_slots, master, moment1, moment2, overflow, clip_on, next_inputs
):
    acts = activations[0]
    tails = tail_grads[0]
    tok_dev, width = acts.shape
    cols = tails.shape[1]
    rows = master.shape[1]
    toks = next_inputs.shape[1]
    own = lax.axis_index("y_lo")

    tokens = next_inputs[0].reshape(toks, NX, NY * NZ, rows)
    tokens = tokens.transpose(2, 0, 1, 3)
    tokens = lax.all_to_all(tokens, YZ, 0, 0, tiled=True)

    terms = gradient_terms(tail_slots[0, 0], tails, acts)
    summed = lax.psum_scatter(
        terms.reshape(NX * NZ * NY * cols, rows), XZ, scatter_dimension=0, tiled=True
    ).reshape(NY, cols, rows)
    mine = lax.dynamic_index_in_dim(summed, own, 0, keepdims=False)
    theirs = lax.dynamic_index_in_dim(summed, 1 - own, 0, keepdims=False)
    total = mine.astype(jnp.float32) + swap_pair(theirs).astype(jnp.float32)
    gradient = total.T * (1.0 / (tok_dev * NX * NY * NZ))

    keep = (overflow[0, 0] == 0).astype(jnp.float32)
    sumsq = lax.psum(keep * jnp.sum(gradient * gradient), EVERY)
    norm_value = jnp.sqrt(sumsq)
    factor = jnp.where(clip_on[0] == 1, 1.0 / jnp.maximum(norm_value, 1.0), 1.0)
    clipped = gradient * factor
    old_master = master[0]
    m_next = beta_one * moment1[0] + (1.0 - beta_one) * clipped
    v_next = beta_two * moment2[0] + (1.0 - beta_two) * (clipped * clipped)
    update = (
        m_next / correct_one / (jnp.sqrt(v_next / correct_two) + adam_eps) + decay_rate * old_master
    )
    updated = jnp.where(keep > 0.5, old_master - learn_rate * update, old_master)
    weights = updated.astype(jnp.bfloat16)

    along_x = lax.all_gather(weights, "x")
    partial = jnp.einsum(
        "gtxr,xrc->gtc", tokens, along_x, preferred_element_type=jnp.float32
    ).astype(jnp.bfloat16)
    parts = lax.all_to_all(partial, YZ, 0, 0, tiled=True)
    result = jnp.sum(parts.astype(jnp.float32), axis=0)
    next_out = (result * (1.0 / math.sqrt(width))).astype(jnp.bfloat16)
    return (updated[None], next_out[None])


def solution(mesh):
    finer = Mesh(mesh.devices.reshape(2, 2, NX, NY, NZ), EVERY)
    return jax.shard_map(
        local,
        mesh=finer,
        in_specs=(
            P(SECTION, DP, None),
            P(SECTION, DP, None),
            P(SECTION, DP, None),
            P(SECTION, DP, None),
            P(SECTION, DP, None),
            P(SECTION, DP, None),
            P(SECTION, DP),
            P(SECTION),
            P(SECTION, DP, None),
        ),
        out_specs=(P(SECTION, DP, None), P(SECTION, DP, None)),
        check_vma=False,
    )
```

```python
import functools
import math

import jax
import jax.numpy as jnp
from jax import lax
from jax.experimental import pallas as pl
from jax.experimental.pallas import tpu as pltpu
from jax.sharding import Mesh
from jax.sharding import PartitionSpec as P

DP = ("x", "y_lo", "z")
YZ = ("y_lo", "z")
SECTION = ("y_hi", "core")
EVERY = SECTION + DP

NX, NY, NZ = 4, 2, 8
COUNT = 4 * NX * NY * NZ


beta_one = 0.9
beta_two = 0.95
correct_one = 1.0 - 0.9**20
correct_two = 1.0 - 0.95**20
adam_eps = 1e-08
decay_rate = 0.1
learn_rate = 0.1

f32 = jnp.float32
bf16 = jnp.bfloat16

ROWS = 128
HALF = 128
PAIR = 2 * HALF


def chunk_terms(pairs, acts):
    if len(acts) == 1:
        step = 4
        for b in range(0, acts[0].shape[1] // ROWS, step):
            part = acts[0][:, b * ROWS : (b + step) * ROWS]
            term = jnp.dot(pairs, part, preferred_element_type=f32)
            for k in range(step):
                yield b + k, term[:, k * ROWS : (k + 1) * ROWS]
    else:
        for b in range(0, len(acts), 2):
            part = jnp.concatenate([acts[b][...], acts[b + 1][...]], axis=1)
            term = jnp.dot(pairs, part, preferred_element_type=f32)
            for k in range(2):
                yield b + k, term[:, k * ROWS : (k + 1) * ROWS]


def first_kernel(where, slots, tails, *refs):
    ax, az = refs[0:1], refs[1 : 1 + NX * NY]
    pairs_ref, xp, xm, zp, zm, placed = refs[1 + NX * NY :]
    tail = tails.shape[0] // slots.shape[0]

    def place(t, carry):
        src = pl.ds(pl.multiple_of(t * tail, tail), tail)
        dst = pl.ds(pl.multiple_of(slots[t] * tail, tail), tail)
        placed[dst, :] = tails[src, :]
        return carry

    lax.fori_loop(0, slots.shape[0], place, 0)
    pairs_ref[...] = placed[...].astype(f32).T.astype(bf16)
    for b, term in chunk_terms(pairs_ref[:PAIR, :], ax):
        xp[b] = term[:HALF].astype(bf16)
        xm[b] = term[HALF:].astype(bf16)
    for b, term in chunk_terms(pairs_ref[PAIR:, :], az):
        zp[b] = term[:HALF].astype(bf16)
        zm[b] = term[HALF:].astype(bf16)


def second_kernel(n, where, pairs, *refs):
    plus, minus = refs[:n], refs[n : 2 * n]
    got_p, got_m, out_p, out_m = refs[2 * n :]
    for b, term in chunk_terms(pairs[...], plus):
        out_p[b, :HALF] = (term[:HALF] + got_p[b].astype(f32)).astype(bf16)
        out_p[b, HALF:] = term[HALF:].astype(bf16)
    for b, term in chunk_terms(pairs[...], minus):
        out_m[b, :HALF] = term[:HALF].astype(bf16)
        out_m[b, HALF:] = (term[HALF:] + got_m[b].astype(f32)).astype(bf16)


def later_kernel(n, where, pairs, *refs):
    plus, minus = refs[:n], refs[n : 2 * n]
    got_p, got_m, out_p, out_m = refs[2 * n :]
    for b, term in chunk_terms(pairs[...], plus):
        out_p[b] = (term + got_p[b].astype(f32)).astype(bf16)
    for b, term in chunk_terms(pairs[...], minus):
        out_m[b] = (term + got_m[b].astype(f32)).astype(bf16)


def last_kernel(n, where, pairs, *refs):
    own = refs[:n]
    got_p, got_m, out = refs[n:]
    for b, term in chunk_terms(pairs[...], own):
        out[b] = term + got_p[b].astype(f32) + got_m[b].astype(f32)


def whole(shape):
    return pl.BlockSpec(shape, lambda i, *s: (0,) * len(shape))


def chunk_specs(axis, tokens, slot):
    if axis == "x":
        width = NY * NZ * ROWS
        return [pl.BlockSpec((tokens, width), lambda i, w, *s: (0, w[slot]))]
    return [
        pl.BlockSpec((tokens, ROWS), lambda i, w, *s, j=j: (0, j * NZ + w[slot]))
        for j in range(NX * NY)
    ]


def blocks_of(axis):
    return NY * NZ if axis == "x" else NX * NY


def gradient_step(kernel, axis, where, pairs, acts, gots, outs, name):
    tokens = acts.shape[0]
    side = 0 if axis == "x" else 1
    specs = [pl.BlockSpec((PAIR, tokens), lambda i, *s: (side, 0))]
    per = chunk_specs(axis, tokens, 0)
    n = len(per)
    chunks = where.shape[0]
    for k in range(chunks):
        specs += chunk_specs(axis, tokens, k)
    specs += [whole(g.shape) for g in gots]
    many = len(outs) > 1
    return pl.pallas_call(
        functools.partial(kernel, n),
        grid_spec=pltpu.PrefetchScalarGridSpec(
            num_scalar_prefetch=1,
            grid=(1,),
            in_specs=specs,
            out_specs=[whole(o.shape) for o in outs] if many else whole(outs[0].shape),
        ),
        out_shape=outs if many else outs[0],
        name=name,
    )(where, pairs, *([acts] * (n * chunks)), *gots)


def shift(x, axis, n, by):
    return lax.ppermute(x, axis, [(i, (i + by) % n) for i in range(n)])


def both(plus, minus, axis, n):
    return shift(plus, axis, n, 1), shift(minus, axis, n, -1)


def spots(*values):
    return jnp.stack(values).astype(jnp.int32)


def sum_terms(slots, tails, acts):
    tokens = acts.shape[0]
    px, pz = lax.axis_index("x"), lax.axis_index("z")
    hx, hz = NX // 2, NZ // 2
    bx, bz = blocks_of("x"), blocks_of("z")
    nz = NX * NY
    half = lambda n: jax.ShapeDtypeStruct((n, HALF, ROWS), bf16)
    full = lambda n, t: jax.ShapeDtypeStruct((n, PAIR, ROWS), t)
    pairs, xp, xm, zp, zm = pl.pallas_call(
        first_kernel,
        grid_spec=pltpu.PrefetchScalarGridSpec(
            num_scalar_prefetch=2,
            grid=(1,),
            in_specs=[whole(tails.shape)]
            + chunk_specs("x", tokens, 0)
            + chunk_specs("z", tokens, 1),
            out_specs=[
                whole((2 * PAIR, tokens)),
                whole((bx, HALF, ROWS)),
                whole((bx, HALF, ROWS)),
                whole((bz, HALF, ROWS)),
                whole((bz, HALF, ROWS)),
            ],
            scratch_shapes=[pltpu.VMEM(tails.shape, tails.dtype)],
        ),
        out_shape=[
            jax.ShapeDtypeStruct((2 * PAIR, tokens), bf16),
            half(bx),
            half(bx),
            half(bz),
            half(bz),
        ],
        name="first_terms",
    )(spots((px + hx) % NX, (pz + hz) % NZ), slots, tails, *([acts] * (1 + nz)))

    def ring(axis, n, pos, plus, minus):
        h, blocks = n // 2, blocks_of(axis)
        gots = both(plus, minus, axis, n)
        for s in range(1, h):
            away = h - s
            where = spots((pos + away) % n, (pos + n - away) % n)
            outs = [full(blocks, bf16)] * 2
            kernel = second_kernel if s == 1 else later_kernel
            sends = gradient_step(
                kernel, axis, where, pairs, acts, gots, outs, f"terms_{axis}{s}"
            )
            gots = both(sends[0], sends[1], axis, n)
        return gradient_step(
            last_kernel, axis, spots(pos), pairs, acts, gots, [full(blocks, f32)], f"terms_{axis}"
        )

    on_x = ring("x", NX, px, xp, xm).reshape(NY, NZ, PAIR, ROWS)
    on_z = ring("z", NZ, pz, zp, zm).reshape(NX, NY, PAIR, ROWS)
    done = ring_rest(on_x, 1, "z", NZ, pz), ring_rest(on_z, 0, "x", NX, px)
    return jnp.concatenate(done, axis=1)


def ring_rest(sums, dim, axis, n, pos):
    h = n // 2
    take = lambda q: lax.dynamic_index_in_dim(sums, (q + n) % n, dim, keepdims=False)
    far = take(pos + h)
    got_p, got_m = both(far[:, :HALF].astype(bf16), far[:, HALF:].astype(bf16), axis, n)
    for s in range(1, h):
        up, down = take(pos + h - s), take(pos - h + s)
        if s == 1:
            zero = jnp.zeros_like(got_p)
            got_p = jnp.concatenate([got_p, zero], axis=1)
            got_m = jnp.concatenate([zero, got_m], axis=1)
        up = (up + got_p.astype(f32)).astype(bf16)
        down = (down + got_m.astype(f32)).astype(bf16)
        got_p, got_m = both(up, down, axis, n)
    return take(pos) + got_p.astype(f32) + got_m.astype(f32)


def local(
    activations, tail_grads, tail_slots, master, moment1, moment2, overflow, clip_on, next_inputs
):
    acts = activations[0]
    tails = tail_grads[0]
    tok_dev, width = acts.shape
    cols = tails.shape[1]
    toks = next_inputs.shape[1]
    px, py = lax.axis_index("x"), lax.axis_index("y_lo")

    mine = next_inputs[0]
    span = width // NX
    tokens = jnp.stack(
        [lax.dynamic_slice_in_dim(mine, (px + r) % NX * span, span, 1) for r in range(NX)]
    )
    tokens = tokens.reshape(NX, toks, NY * NZ, ROWS).transpose(2, 1, 0, 3)
    tokens = tokens.reshape(NY * NZ, toks, NX * ROWS)
    tokens = lax.all_to_all(tokens, YZ, 0, 0, tiled=True)

    summed = sum_terms(tail_slots[0, 0], tails, acts)
    keeps = lax.dynamic_index_in_dim(summed, py, 0, keepdims=False)
    gives = lax.dynamic_index_in_dim(summed, 1 - py, 0, keepdims=False)
    total = keeps + shift(gives.astype(bf16), "y_lo", NY, 1).astype(f32)
    gradient = total.T * (1.0 / (tok_dev * NX * NY * NZ))

    keep = (overflow[0, 0] == 0).astype(f32)
    part_sq = jnp.broadcast_to(keep * jnp.sum(gradient * gradient), (COUNT, 1, 128))
    sumsq = jnp.sum(lax.all_to_all(part_sq, EVERY, 0, 0, tiled=True), axis=0)[0, 0]
    norm_value = jnp.sqrt(sumsq)
    factor = jnp.where(clip_on[0] == 1, 1.0 / jnp.maximum(norm_value, 1.0), 1.0)
    clipped = gradient * factor
    old_master = master[0]
    m_next = beta_one * moment1[0] + (1.0 - beta_one) * clipped
    v_next = beta_two * moment2[0] + (1.0 - beta_two) * (clipped * clipped)
    update = (
        m_next / correct_one / (jnp.sqrt(v_next / correct_two) + adam_eps) + decay_rate * old_master
    )
    updated = jnp.where(keep > 0.5, old_master - learn_rate * update, old_master)
    weights = updated.astype(bf16)

    along_x = jnp.concatenate(
        [weights] + [shift(weights, "x", NX, -r) for r in range(1, NX)], axis=0
    )
    partial = jnp.einsum("gtk,kc->gtc", tokens, along_x, preferred_element_type=f32).astype(bf16)
    parts = lax.all_to_all(partial, YZ, 0, 0, tiled=True)
    result = jnp.sum(parts.astype(f32), axis=0)
    next_out = (result * (1.0 / math.sqrt(width))).astype(bf16)
    return (updated[None], next_out[None])


def solution(mesh):
    finer = Mesh(mesh.devices.reshape(2, 2, NX, NY, NZ), EVERY)
    return jax.shard_map(
        local,
        mesh=finer,
        in_specs=(
            P(SECTION, DP, None),
            P(SECTION, DP, None),
            P(SECTION, DP, None),
            P(SECTION, DP, None),
            P(SECTION, DP, None),
            P(SECTION, DP, None),
            P(SECTION, DP),
            P(SECTION),
            P(SECTION, DP, None),
        ),
        out_specs=(P(SECTION, DP, None), P(SECTION, DP, None)),
        check_vma=False,
    )
```

```python
import functools
import math

import jax
import jax.numpy as jnp
from jax import lax
from jax.experimental import pallas as pl
from jax.experimental.pallas import tpu as pltpu
from jax.sharding import Mesh
from jax.sharding import PartitionSpec as P

DP = ("x", "y_lo", "z")
YZ = ("y_lo", "z")
SECTION = ("y_hi", "core")
EVERY = SECTION + DP

NX, NY, NZ = 4, 2, 8


beta_one = 0.9
beta_two = 0.95
correct_one = 1.0 - 0.9**20
correct_two = 1.0 - 0.95**20
adam_eps = 1e-08
decay_rate = 0.1
learn_rate = 0.1

f32 = jnp.float32
bf16 = jnp.bfloat16

ROWS = 128
X_COLS, Z_COLS = 192, 320
X_HALF, Z_HALF = X_COLS // 2, Z_COLS // 2
Z_WIDE = NX * ROWS


def column(x, y, z):
    return pl.multiple_of((x * (NY * NZ) + y * NZ + z) * ROWS, ROWS)


def x_terms(where, away, pairs, acts):
    owner = lax.rem(where[0] + away, NX)
    step = 4
    for b in range(0, NY * NZ, step):
        part = acts[:, pl.ds(column(owner, 0, b), step * ROWS)]
        term = jnp.dot(pairs, part, preferred_element_type=f32)
        for k in range(step):
            yield b + k, term[:, k * ROWS : (k + 1) * ROWS]


def side_columns(where, side, away, acts, turn=0):
    owner = lax.rem(where[1] + away, NZ)
    xs = [lax.rem(turn + k, NX) for k in range(NX)]
    return jnp.concatenate([acts[:, pl.ds(column(x, side, owner), ROWS)] for x in xs], axis=1)


def partner_pairs(joined):
    tail = joined[joined.shape[1] // 2 :, :]
    half = tail.shape[1] // 2
    return jnp.concatenate([tail[:, :half], tail[:, half:]], axis=0)


def z_terms(where, away, pairs, acts, joined, part):
    own = jnp.dot(
        pairs[...], side_columns(where, where[2], away, acts), preferred_element_type=f32
    )
    term = own + jnp.dot(partner_pairs(joined), part, preferred_element_type=f32)
    for k in range(NX):
        yield k, term[:, k * ROWS : (k + 1) * ROWS]


def first_kernel(where, slots, tails, acts, x_pairs, z_pairs, xp, xm, *refs):
    gives, placed = refs[:-1], refs[-1]
    tail = tails.shape[0] // slots.shape[0]

    def place(t, carry):
        src = pl.ds(pl.multiple_of(t * tail, tail), tail)
        dst = pl.ds(pl.multiple_of(slots[t] * tail, tail), tail)
        placed[dst, :] = tails[src, :]
        return carry

    lax.fori_loop(0, slots.shape[0], place, 0)
    pairs = placed[...].astype(f32).T.astype(bf16)
    x_pairs[...] = pairs[:X_COLS]
    z_pairs[...] = pairs[X_COLS:]
    tokens = acts.shape[0]
    for k, give in enumerate(gives):
        away = NZ // 2 - k
        for n, far in enumerate((away,) if away in (0, NZ // 2) else (away, NZ - away)):
            give[:tokens, n * Z_WIDE : (n + 1) * Z_WIDE] = side_columns(
                where, 1 - where[2], far, acts
            )
    gives[0][tokens:, :tokens] = pairs[X_COLS : X_COLS + Z_HALF]
    gives[0][tokens:, tokens:] = pairs[X_COLS + Z_HALF :]
    for b, term in x_terms(where, NX // 2, pairs[:X_COLS], acts):
        xp[b] = term[:X_HALF].astype(bf16)
        xm[b] = term[X_HALF:].astype(bf16)


def second_x_kernel(where, pairs, acts, got_p, got_m, out_p, out_m):
    for b, term in x_terms(where, 1, pairs[...], acts):
        out_p[b, :X_HALF] = (term[:X_HALF] + got_p[b].astype(f32)).astype(bf16)
        out_p[b, X_HALF:] = term[X_HALF:].astype(bf16)
    for b, term in x_terms(where, NX - 1, pairs[...], acts):
        out_m[b, :X_HALF] = term[:X_HALF].astype(bf16)
        out_m[b, X_HALF:] = (term[X_HALF:] + got_m[b].astype(f32)).astype(bf16)


def last_x_kernel(where, pairs, acts, got_p, got_m, out):
    for b, term in x_terms(where, 0, pairs[...], acts):
        out[b] = (term + got_p[b].astype(f32) + got_m[b].astype(f32)).astype(bf16)


def first_z_kernel(where, pairs, acts, joined, out_p, out_m):
    part = joined[: acts.shape[0], :]
    for k, term in z_terms(where, NZ // 2, pairs, acts, joined, part):
        out_p[k] = term[:Z_HALF].astype(bf16)
        out_m[k] = term[Z_HALF:].astype(bf16)


def later_z_kernel(s, where, pairs, acts, joined, part, got_p, got_m, out_p, out_m):
    away = NZ // 2 - s
    for k, term in z_terms(where, away, pairs, acts, joined, part[:, :Z_WIDE]):
        if s == 1:
            out_p[k, :Z_HALF] = (term[:Z_HALF] + got_p[k].astype(f32)).astype(bf16)
            out_p[k, Z_HALF:] = term[Z_HALF:].astype(bf16)
        else:
            out_p[k] = (term + got_p[k].astype(f32)).astype(bf16)
    for k, term in z_terms(where, NZ - away, pairs, acts, joined, part[:, Z_WIDE:]):
        if s == 1:
            out_m[k, :Z_HALF] = term[:Z_HALF].astype(bf16)
            out_m[k, Z_HALF:] = (term[Z_HALF:] + got_m[k].astype(f32)).astype(bf16)
        else:
            out_m[k] = (term + got_m[k].astype(f32)).astype(bf16)


def last_z_kernel(where, pairs, acts, joined, part, got_p, got_m, own, *sends):
    mine = jnp.dot(
        pairs[...], side_columns(where, where[2], 0, acts, where[0]), preferred_element_type=f32
    )
    xs = [lax.rem(where[0] + r, NX) for r in range(NX)]
    parts = [part[:, pl.ds(pl.multiple_of(x * ROWS, ROWS), ROWS)] for x in xs]
    term = mine + jnp.dot(
        partner_pairs(joined), jnp.concatenate(parts, axis=1), preferred_element_type=f32
    )
    for r, x in enumerate(xs):
        total = term[:, r * ROWS : (r + 1) * ROWS] + got_p[x].astype(f32) + got_m[x].astype(f32)
        if r == 0:
            own[...] = total
        else:
            sends[r - 1][...] = total.astype(bf16)


def gradient_kernel(scale, overflow, on_x, own, *refs):
    gots, (grad, squares) = refs[: NX - 1], refs[NX - 1 :]
    first = on_x[0].astype(f32)
    for k in range(1, on_x.shape[0]):
        first += on_x[k].astype(f32)
    second = own[...]
    for got in gots:
        second += got[...].astype(f32)
    total = jnp.concatenate([first, second], axis=0).T * scale
    grad[...] = total
    kept = jnp.where(overflow[0, 0] == 0, 1.0, 0.0)
    squares[...] = jnp.broadcast_to(jnp.sum(total * total) * kept, squares.shape)


def tokens_kernel(where, mine, out):
    for r in range(NX):
        owner = lax.rem(where[0] + r, NX)
        for g in range(NY * NZ):
            start = pl.multiple_of((owner * (NY * NZ) + g) * ROWS, ROWS)
            out[g, :, r * ROWS : (r + 1) * ROWS] = mine[:, pl.ds(start, ROWS)]


def near(x):
    return pltpu.with_memory_space_constraint(x, pltpu.VMEM)


SCALARS = pl.BlockSpec(memory_space=pltpu.SMEM)
GRANT = pltpu.CompilerParams(vmem_limit_bytes=8 * 2**20)
NEAR = pl.BlockSpec(memory_space=pltpu.VMEM)


def on_core(kernel, scalars, arrays, outs, scratch=()):
    return pl.pallas_call(
        kernel,
        in_specs=[SCALARS] * len(scalars) + [NEAR] * len(arrays),
        out_specs=[NEAR] * len(outs),
        out_shape=list(outs),
        scratch_shapes=scratch,
        compiler_params=GRANT,
    )(*scalars, *[near(a) for a in arrays])


def shift(x, axis, n, by):
    return lax.ppermute(x, axis, [(i, (i + by) % n) for i in range(n)])


def both(plus, minus, axis, n):
    return shift(plus, axis, n, 1), shift(minus, axis, n, -1)


def swap_side(x):
    return shift(x, "y_lo", NY, 1)


def sum_terms(where, slots, tails, acts):
    tokens = acts.shape[0]
    x_blocks = NY * NZ
    two = lambda *shape: [pltpu.VMEM(shape, bf16)] * 2
    wide = [Z_WIDE] + [2 * Z_WIDE] * (NZ // 2 - 1) + [Z_WIDE]
    tall = [tokens + Z_HALF] + [tokens] * (NZ // 2)
    outs = [pltpu.VMEM((X_COLS, tokens), bf16), pltpu.VMEM((Z_COLS, tokens), bf16)]
    outs += two(x_blocks, X_HALF, ROWS)
    outs += [pltpu.VMEM(shape, bf16) for shape in zip(tall, wide)]
    x_pairs, z_pairs, xp, xm, *gives = on_core(
        first_kernel, [where, slots], [tails, acts], outs, [pltpu.VMEM(tails.shape, bf16)]
    )

    gots = both(xp, xm, "x", NX)
    joined, *parts = [swap_side(give) for give in gives]

    sends = on_core(second_x_kernel, [where], [x_pairs, acts, *gots], two(x_blocks, X_COLS, ROWS))
    gots = both(*sends, "x", NX)
    (on_x,) = on_core(
        last_x_kernel,
        [where],
        [x_pairs, acts, *gots],
        [jax.ShapeDtypeStruct((x_blocks, X_COLS, ROWS), bf16)],
    )
    on_x = lax.all_to_all(on_x, YZ, 0, 0, tiled=True)

    sends = on_core(first_z_kernel, [where], [z_pairs, acts, joined], two(NX, Z_HALF, ROWS))
    gots = both(*sends, "z", NZ)
    for s in range(1, NZ // 2):
        sends = on_core(
            functools.partial(later_z_kernel, s),
            [where],
            [z_pairs, acts, joined, parts[s - 1], *gots],
            two(NX, Z_COLS, ROWS),
        )
        gots = both(*sends, "z", NZ)
    piece = lambda t: pltpu.VMEM((Z_COLS, ROWS), t)
    own, *sends = on_core(
        last_z_kernel,
        [where],
        [z_pairs, acts, joined, parts[-1], *gots],
        [piece(f32)] + [piece(bf16)] * (NX - 1),
    )
    gots = [shift(send, "x", NX, r + 1) for r, send in enumerate(sends)]
    return on_x, own, gots


def local(
    activations, tail_grads, tail_slots, master, moment1, moment2, overflow, clip_on, next_inputs
):
    acts = activations[0]
    tails = tail_grads[0]
    tok_dev, width = acts.shape
    toks = next_inputs.shape[1]
    where = jnp.stack([lax.axis_index(a) for a in ("x", "z", "y_lo")]).astype(jnp.int32)

    tokens = jax.ShapeDtypeStruct((NY * NZ, toks, NX * ROWS), bf16)
    (tokens,) = on_core(tokens_kernel, [where], [next_inputs[0]], [tokens])
    tokens = lax.all_to_all(tokens, YZ, 0, 0, tiled=True)

    on_x, own, gots = sum_terms(where, tail_slots[0, 0], tails, acts)
    gradient, part_sq = on_core(
        functools.partial(gradient_kernel, 1.0 / (tok_dev * NX * NY * NZ)),
        [overflow],
        [on_x, own, *gots],
        [pltpu.VMEM((ROWS, X_COLS + Z_COLS), f32), pltpu.VMEM((1, 128), f32)],
    )
    keep = (overflow[0, 0] == 0).astype(f32)
    part_sq = part_sq + shift(part_sq, "core", 2, 1)
    by_y = [lax.ppermute(part_sq, ("y_hi", "y_lo"), [(i, i ^ m) for i in range(4)]) for m in (1, 2, 3)]
    part_sq = (part_sq + by_y[0]) + (by_y[1] + by_y[2])
    part_sq = jnp.broadcast_to(part_sq[None], (NX * NZ, 1, 128))
    sumsq = jnp.sum(lax.all_to_all(part_sq, ("x", "z"), 0, 0, tiled=True), axis=0)[0, 0]
    norm_value = jnp.sqrt(sumsq)
    factor = jnp.where(clip_on[0] == 1, 1.0 / jnp.maximum(norm_value, 1.0), 1.0)
    clipped = gradient * factor
    old_master = master[0]
    m_next = beta_one * moment1[0] + (1.0 - beta_one) * clipped
    v_next = beta_two * moment2[0] + (1.0 - beta_two) * (clipped * clipped)
    update = (
        m_next / correct_one / (jnp.sqrt(v_next / correct_two) + adam_eps) + decay_rate * old_master
    )
    updated = jnp.where(keep > 0.5, old_master - learn_rate * update, old_master)
    weights = updated.astype(bf16)

    along_x = jnp.concatenate(
        [weights] + [shift(weights, "x", NX, -r) for r in range(1, NX)], axis=0
    )
    partial = jnp.einsum("gtk,kc->gtc", tokens, along_x, preferred_element_type=f32).astype(bf16)
    parts = lax.all_to_all(partial, YZ, 0, 0, tiled=True)
    result = jnp.sum(parts.astype(f32), axis=0)
    next_out = (result * (1.0 / math.sqrt(width))).astype(bf16)
    return (updated[None], next_out[None])


def solution(mesh):
    finer = Mesh(mesh.devices.reshape(2, 2, NX, NY, NZ), EVERY)
    return jax.shard_map(
        local,
        mesh=finer,
        in_specs=(
            P(SECTION, DP, None),
            P(SECTION, DP, None),
            P(SECTION, DP, None),
            P(SECTION, DP, None),
            P(SECTION, DP, None),
            P(SECTION, DP, None),
            P(SECTION, DP),
            P(SECTION),
            P(SECTION, DP, None),
        ),
        out_specs=(P(SECTION, DP, None), P(SECTION, DP, None)),
        check_vma=False,
    )
```

```python
import functools
import math

import jax
import jax.numpy as jnp
from jax import lax
from jax.experimental import pallas as pl
from jax.experimental.pallas import tpu as pltpu
from jax.sharding import Mesh
from jax.sharding import PartitionSpec as P

DP = ("x", "y_lo", "z")
YZ = ("y_lo", "z")
SECTION = ("y_hi", "core")
EVERY = SECTION + DP

NX, NY, NZ = 4, 2, 8


beta_one = 0.9
beta_two = 0.95
correct_one = 1.0 - 0.9**20
correct_two = 1.0 - 0.95**20
adam_eps = 1e-08
decay_rate = 0.1
learn_rate = 0.1

f32 = jnp.float32
bf16 = jnp.bfloat16

ROWS = 128
X_COLS, Z_COLS = 192, 320
X_HALF, Z_HALF = X_COLS // 2, Z_COLS // 2
Z_WIDE = NX * ROWS
EXTRA = 16


def column(x, y, z):
    return pl.multiple_of((x * (NY * NZ) + y * NZ + z) * ROWS, ROWS)


def x_terms(where, away, pairs, acts):
    owner = lax.rem(where[0] + away, NX)
    step = 4
    for b in range(0, NY * NZ, step):
        part = acts[:, pl.ds(column(owner, 0, b), step * ROWS)]
        term = jnp.dot(pairs, part, preferred_element_type=f32)
        for k in range(step):
            yield b + k, term[:, k * ROWS : (k + 1) * ROWS]


def side_columns(where, side, away, acts, turn=0):
    owner = lax.rem(where[1] + away, NZ)
    xs = [lax.rem(turn + k, NX) for k in range(NX)]
    return jnp.concatenate([acts[:, pl.ds(column(x, side, owner), ROWS)] for x in xs], axis=1)


def partner_pairs(joined):
    tail = joined[joined.shape[1] // 2 :, :]
    half = tail.shape[1] // 2
    return jnp.concatenate([tail[:, :half], tail[:, half:]], axis=0)


def z_terms(where, away, pairs, acts, joined, part):
    own = jnp.dot(
        pairs[...], side_columns(where, where[2], away, acts), preferred_element_type=f32
    )
    term = own + jnp.dot(partner_pairs(joined), part, preferred_element_type=f32)
    for k in range(NX):
        yield k, term[:, k * ROWS : (k + 1) * ROWS]


def first_kernel(where, slots, tails, acts, x_pairs, z_pairs, xp, xm, *refs):
    gives, placed = refs[:-1], refs[-1]
    tail = tails.shape[0] // slots.shape[0]

    def place(t, carry):
        src = pl.ds(pl.multiple_of(t * tail, tail), tail)
        dst = pl.ds(pl.multiple_of(slots[t] * tail, tail), tail)
        placed[dst, :] = tails[src, :]
        return carry

    lax.fori_loop(0, slots.shape[0], place, 0)
    pairs = placed[...].astype(f32).T.astype(bf16)
    x_pairs[...] = pairs[:X_COLS]
    z_pairs[...] = pairs[X_COLS:]
    tokens = acts.shape[0]
    for k, give in enumerate(gives):
        away = NZ // 2 - k
        for n, far in enumerate((away,) if away in (0, NZ // 2) else (away, NZ - away)):
            give[:tokens, n * Z_WIDE : (n + 1) * Z_WIDE] = side_columns(
                where, 1 - where[2], far, acts
            )
    gives[0][tokens:, :tokens] = pairs[X_COLS : X_COLS + Z_HALF]
    gives[0][tokens:, tokens:] = pairs[X_COLS + Z_HALF :]
    for b, term in x_terms(where, NX // 2, pairs[:X_COLS], acts):
        xp[b] = term[:X_HALF].astype(bf16)
        xm[b] = term[X_HALF:].astype(bf16)


def second_x_kernel(where, pairs, acts, got_p, got_m, out_p, out_m):
    for b, term in x_terms(where, 1, pairs[...], acts):
        out_p[b, :X_HALF] = (term[:X_HALF] + got_p[b].astype(f32)).astype(bf16)
        out_p[b, X_HALF:] = term[X_HALF:].astype(bf16)
    for b, term in x_terms(where, NX - 1, pairs[...], acts):
        out_m[b, :X_HALF] = term[:X_HALF].astype(bf16)
        out_m[b, X_HALF:] = (term[X_HALF:] + got_m[b].astype(f32)).astype(bf16)


def last_x_kernel(where, pairs, acts, got_p, got_m, out):
    for b, term in x_terms(where, 0, pairs[...], acts):
        out[b] = (term + got_p[b].astype(f32) + got_m[b].astype(f32)).astype(bf16)


def first_z_kernel(where, pairs, acts, joined, out_p, out_m):
    part = joined[: acts.shape[0], :]
    for k, term in z_terms(where, NZ // 2, pairs, acts, joined, part):
        out_p[k] = term[:Z_HALF].astype(bf16)
        out_m[k] = term[Z_HALF:].astype(bf16)


def later_z_kernel(s, where, pairs, acts, joined, part, got_p, got_m, out_p, out_m):
    away = NZ // 2 - s
    for k, term in z_terms(where, away, pairs, acts, joined, part[:, :Z_WIDE]):
        if s == 1:
            out_p[k, :Z_HALF] = (term[:Z_HALF] + got_p[k].astype(f32)).astype(bf16)
            out_p[k, Z_HALF:] = term[Z_HALF:].astype(bf16)
        else:
            out_p[k] = (term + got_p[k].astype(f32)).astype(bf16)
    for k, term in z_terms(where, NZ - away, pairs, acts, joined, part[:, Z_WIDE:]):
        if s == 1:
            out_m[k, :Z_HALF] = term[:Z_HALF].astype(bf16)
            out_m[k, Z_HALF:] = (term[Z_HALF:] + got_m[k].astype(f32)).astype(bf16)
        else:
            out_m[k] = (term + got_m[k].astype(f32)).astype(bf16)


def own_z_kernel(where, pairs, acts, joined, part, out):
    mine = jnp.dot(
        pairs[...], side_columns(where, where[2], 0, acts, where[0]), preferred_element_type=f32
    )
    xs = [lax.rem(where[0] + r, NX) for r in range(NX)]
    parts = [part[:, pl.ds(pl.multiple_of(x * ROWS, ROWS), ROWS)] for x in xs]
    out[...] = mine + jnp.dot(
        partner_pairs(joined), jnp.concatenate(parts, axis=1), preferred_element_type=f32
    )


def last_z_kernel(where, term, got_p, got_m, own, *sends):
    for r in range(NX):
        x = lax.rem(where[0] + r, NX)
        total = term[:, r * ROWS : (r + 1) * ROWS] + got_p[x].astype(f32) + got_m[x].astype(f32)
        if r == 0:
            own[...] = total
        else:
            sends[r - 1][...] = total.astype(bf16)


def gradient_kernel(scale, overflow, on_x, own, *refs):
    gots, (grad, squares) = refs[: NX - 1], refs[NX - 1 :]
    first = on_x[0].astype(f32)
    for k in range(1, on_x.shape[0]):
        first += on_x[k].astype(f32)
    second = own[...]
    for got in gots:
        second += got[...].astype(f32)
    total = jnp.concatenate([first, second], axis=0).T * scale
    grad[...] = total
    kept = jnp.where(overflow[0, 0] == 0, 1.0, 0.0)
    squares[...] = jnp.broadcast_to(jnp.sum(total * total) * kept, squares.shape)


def tokens_kernel(where, mine, out):
    for r in range(NX):
        owner = lax.rem(where[0] + r, NX)
        for g in range(NY * NZ):
            start = pl.multiple_of((owner * (NY * NZ) + g) * ROWS, ROWS)
            out[g, : mine.shape[0], r * ROWS : (r + 1) * ROWS] = mine[:, pl.ds(start, ROWS)]
    out[:, mine.shape[0] :, :] = jnp.zeros((out.shape[0], EXTRA, out.shape[2]), out.dtype)


def near(x):
    return pltpu.with_memory_space_constraint(x, pltpu.VMEM)


SCALARS = pl.BlockSpec(memory_space=pltpu.SMEM)
GRANT = pltpu.CompilerParams(vmem_limit_bytes=8 * 2**20)
NEAR = pl.BlockSpec(memory_space=pltpu.VMEM)


def on_core(kernel, scalars, arrays, outs, scratch=()):
    return pl.pallas_call(
        kernel,
        in_specs=[SCALARS] * len(scalars) + [NEAR] * len(arrays),
        out_specs=[NEAR] * len(outs),
        out_shape=list(outs),
        scratch_shapes=scratch,
        compiler_params=GRANT,
    )(*scalars, *[near(a) for a in arrays])


def shift(x, axis, n, by):
    return lax.ppermute(x, axis, [(i, (i + by) % n) for i in range(n)])


def both(plus, minus, axis, n):
    return shift(plus, axis, n, 1), shift(minus, axis, n, -1)


def swap_side(x):
    return shift(x, "y_lo", NY, 1)


def sum_terms(where, slots, tails, acts):
    tokens = acts.shape[0]
    x_blocks = NY * NZ
    two = lambda *shape: [pltpu.VMEM(shape, bf16)] * 2
    wide = [Z_WIDE] + [2 * Z_WIDE] * (NZ // 2 - 1) + [Z_WIDE]
    tall = [tokens + Z_HALF] + [tokens] * (NZ // 2)
    outs = [pltpu.VMEM((X_COLS, tokens), bf16), pltpu.VMEM((Z_COLS, tokens), bf16)]
    outs += two(x_blocks, X_HALF, ROWS)
    outs += [pltpu.VMEM(shape, bf16) for shape in zip(tall, wide)]
    x_pairs, z_pairs, xp, xm, *gives = on_core(
        first_kernel, [where, slots], [tails, acts], outs, [pltpu.VMEM(tails.shape, bf16)]
    )

    gots = both(xp, xm, "x", NX)
    joined, *parts = [swap_side(give) for give in gives]

    sends = on_core(second_x_kernel, [where], [x_pairs, acts, *gots], two(x_blocks, X_COLS, ROWS))
    gots = both(*sends, "x", NX)
    (on_x,) = on_core(
        last_x_kernel,
        [where],
        [x_pairs, acts, *gots],
        [jax.ShapeDtypeStruct((x_blocks, X_COLS, ROWS), bf16)],
    )
    on_x = lax.all_to_all(on_x, YZ, 0, 0, tiled=True)

    sends = on_core(first_z_kernel, [where], [z_pairs, acts, joined], two(NX, Z_HALF, ROWS))
    gots = both(*sends, "z", NZ)
    for s in range(1, NZ // 2):
        sends = on_core(
            functools.partial(later_z_kernel, s),
            [where],
            [z_pairs, acts, joined, parts[s - 1], *gots],
            two(NX, Z_COLS, ROWS),
        )
        gots = both(*sends, "z", NZ)
    piece = lambda t: pltpu.VMEM((Z_COLS, ROWS), t)
    (term,) = on_core(
        own_z_kernel,
        [where],
        [z_pairs, acts, joined, parts[-1]],
        [pltpu.VMEM((Z_COLS, Z_WIDE), f32)],
    )
    own, *sends = on_core(
        last_z_kernel, [where], [term, *gots], [piece(f32)] + [piece(bf16)] * (NX - 1)
    )
    gots = [shift(send, "x", NX, r + 1) for r, send in enumerate(sends)]
    return on_x, own, gots


def local(
    activations, tail_grads, tail_slots, master, moment1, moment2, overflow, clip_on, next_inputs
):
    acts = activations[0]
    tails = tail_grads[0]
    tok_dev, width = acts.shape
    toks = next_inputs.shape[1]
    where = jnp.stack([lax.axis_index(a) for a in ("x", "z", "y_lo")]).astype(jnp.int32)

    tokens = jax.ShapeDtypeStruct((NY * NZ, toks + EXTRA, NX * ROWS), bf16)
    (tokens,) = on_core(tokens_kernel, [where], [next_inputs[0]], [tokens])

    on_x, own, gots = sum_terms(where, tail_slots[0, 0], tails, acts)
    gradient, part_sq = on_core(
        functools.partial(gradient_kernel, 1.0 / (tok_dev * NX * NY * NZ)),
        [overflow],
        [on_x, own, *gots],
        [pltpu.VMEM((ROWS, X_COLS + Z_COLS), f32), pltpu.VMEM((1, 128), f32)],
    )
    keep = (overflow[0, 0] == 0).astype(f32)
    others = ("y_hi", "core", "x")
    part_sq = jnp.broadcast_to(part_sq[None], (4 * NX, 1, ROWS))
    part_sq = jnp.sum(lax.all_to_all(part_sq, others, 0, 0, tiled=True), axis=0)[0, 0]
    high = lax.reduce_precision(part_sq, 8, 7)
    middle = lax.reduce_precision(part_sq - high, 8, 7)
    pieces = jnp.stack([high, middle, part_sq - high - middle, 0.0 * high])
    pieces = jnp.broadcast_to(jnp.repeat(pieces, ROWS)[None, None], (NY * NZ, EXTRA, NX * ROWS))
    tokens = lax.dynamic_update_slice(tokens, pieces.astype(bf16), (0, toks, 0))
    tokens = lax.all_to_all(tokens, YZ, 0, 0, tiled=True)
    pieces = jnp.sum(tokens[:, toks, :].astype(f32), axis=0)
    tokens = tokens[:, :toks]
    sumsq = pieces[0] + pieces[ROWS] + pieces[2 * ROWS]
    norm_value = jnp.sqrt(sumsq)
    factor = jnp.where(clip_on[0] == 1, 1.0 / jnp.maximum(norm_value, 1.0), 1.0)
    clipped = gradient * factor
    old_master = master[0]
    m_next = beta_one * moment1[0] + (1.0 - beta_one) * clipped
    v_next = beta_two * moment2[0] + (1.0 - beta_two) * (clipped * clipped)
    update = (
        m_next / correct_one / (jnp.sqrt(v_next / correct_two) + adam_eps) + decay_rate * old_master
    )
    updated = jnp.where(keep > 0.5, old_master - learn_rate * update, old_master)
    weights = updated.astype(bf16)

    along_x = jnp.concatenate(
        [weights] + [shift(weights, "x", NX, -r) for r in range(1, NX)], axis=0
    )
    partial = jnp.einsum("gtk,kc->gtc", tokens, along_x, preferred_element_type=f32).astype(bf16)
    parts = lax.all_to_all(partial, YZ, 0, 0, tiled=True)
    result = jnp.sum(parts.astype(f32), axis=0)
    next_out = (result * (1.0 / math.sqrt(width))).astype(bf16)
    return (updated[None], next_out[None])


def solution(mesh):
    finer = Mesh(mesh.devices.reshape(2, 2, NX, NY, NZ), EVERY)
    return jax.shard_map(
        local,
        mesh=finer,
        in_specs=(
            P(SECTION, DP, None),
            P(SECTION, DP, None),
            P(SECTION, DP, None),
            P(SECTION, DP, None),
            P(SECTION, DP, None),
            P(SECTION, DP, None),
            P(SECTION, DP),
            P(SECTION),
            P(SECTION, DP, None),
        ),
        out_specs=(P(SECTION, DP, None), P(SECTION, DP, None)),
        check_vma=False,
    )
```

```python
import functools
import math

import jax
import jax.numpy as jnp
from jax import lax
from jax.experimental import pallas as pl
from jax.experimental.pallas import tpu as pltpu
from jax.sharding import Mesh
from jax.sharding import PartitionSpec as P

DP = ("x", "y_lo", "z")
YZ = ("y_lo", "z")
SECTION = ("y_hi", "core")
EVERY = SECTION + DP

NX, NY, NZ = 4, 2, 8
TAILS = 4


beta_one = 0.9
beta_two = 0.95
correct_one = 1.0 - 0.9**20
correct_two = 1.0 - 0.95**20
adam_eps = 1e-08
decay_rate = 0.1
learn_rate = 0.1

f32 = jnp.float32
bf16 = jnp.bfloat16

ROWS = 128
COLS = 512
HALF = COLS // 2
Z_WIDE = NX * ROWS


def column(x, y, z):
    return pl.multiple_of((x * (NY * NZ) + y * NZ + z) * ROWS, ROWS)


def side_columns(where, side, away, acts, turn=0):
    owner = lax.rem(where[1] + away, NZ)
    xs = [lax.rem(turn + k, NX) for k in range(NX)]
    return jnp.concatenate([acts[:, pl.ds(column(x, side, owner), ROWS)] for x in xs], axis=1)


def partner_pairs(joined):
    tail = joined[joined.shape[1] // 2 :, :]
    half = tail.shape[1] // 2
    return jnp.concatenate([tail[:, :half], tail[:, half:]], axis=0)


def z_terms(where, away, pairs, acts, joined, part):
    own = jnp.dot(
        pairs[...], side_columns(where, where[2], away, acts), preferred_element_type=f32
    )
    term = own + jnp.dot(partner_pairs(joined), part, preferred_element_type=f32)
    for k in range(NX):
        yield k, term[:, k * ROWS : (k + 1) * ROWS]


def first_kernel(where, tails, *refs):
    acts, (pairs, give, placed) = refs[:NX], refs[NX:]
    tail = tails.shape[0] // TAILS

    def place(t, carry):
        src = pl.ds(pl.multiple_of(t * tail, tail), tail)
        dst = pl.ds(pl.multiple_of(where[3 + t] * tail, tail), tail)
        placed[dst, :] = tails[src, :]
        return carry

    lax.fori_loop(0, TAILS, place, 0)
    tokens = tails.shape[0]
    value = placed[...].astype(f32).T.astype(bf16)
    pairs[...] = value
    for k in range(NX):
        give[:tokens, k * ROWS : (k + 1) * ROWS] = acts[k][...]
    give[tokens:, :tokens] = value[:HALF]
    give[tokens:, tokens:] = value[HALF:]


def pack_kernel(where, acts, *gives):
    for k, give in enumerate(gives):
        away = NZ // 2 - 1 - k
        for n, far in enumerate((away, NZ - away) if away else (0,)):
            give[:, n * Z_WIDE : (n + 1) * Z_WIDE] = side_columns(where, 1 - where[2], far, acts)


def first_z_kernel(where, pairs, acts, joined, out_p, out_m):
    part = joined[: acts.shape[0], :]
    for k, term in z_terms(where, NZ // 2, pairs, acts, joined, part):
        out_p[k] = term[:HALF].astype(bf16)
        out_m[k] = term[HALF:].astype(bf16)


def later_z_kernel(s, where, pairs, acts, joined, part, got_p, got_m, out_p, out_m):
    away = NZ // 2 - s
    for k, term in z_terms(where, away, pairs, acts, joined, part[:, :Z_WIDE]):
        if s == 1:
            out_p[k, :HALF] = (term[:HALF] + got_p[k].astype(f32)).astype(bf16)
            out_p[k, HALF:] = term[HALF:].astype(bf16)
        else:
            out_p[k] = (term + got_p[k].astype(f32)).astype(bf16)
    for k, term in z_terms(where, NZ - away, pairs, acts, joined, part[:, Z_WIDE:]):
        if s == 1:
            out_m[k, :HALF] = term[:HALF].astype(bf16)
            out_m[k, HALF:] = (term[HALF:] + got_m[k].astype(f32)).astype(bf16)
        else:
            out_m[k] = (term + got_m[k].astype(f32)).astype(bf16)


def own_z_kernel(where, pairs, acts, joined, part, out):
    mine = jnp.dot(
        pairs[...], side_columns(where, where[2], 0, acts, where[0]), preferred_element_type=f32
    )
    xs = [lax.rem(where[0] + r, NX) for r in range(NX)]
    parts = [part[:, pl.ds(pl.multiple_of(x * ROWS, ROWS), ROWS)] for x in xs]
    out[...] = mine + jnp.dot(
        partner_pairs(joined), jnp.concatenate(parts, axis=1), preferred_element_type=f32
    )


def last_z_kernel(where, term, got_p, got_m, own, *sends):
    for r in range(NX):
        x = lax.rem(where[0] + r, NX)
        total = term[:, r * ROWS : (r + 1) * ROWS] + got_p[x].astype(f32) + got_m[x].astype(f32)
        if r == 0:
            own[...] = total
        else:
            sends[r - 1][...] = total.astype(bf16)


def gradient_kernel(scale, overflow, own, *refs):
    gots, (grad, squares) = refs[: NX - 1], refs[NX - 1 :]
    total = own[...]
    for got in gots:
        total += got[...].astype(f32)
    total = total.T * scale
    grad[...] = total
    kept = jnp.where(overflow[0, 0] == 0, 1.0, 0.0)
    squares[...] = jnp.broadcast_to(jnp.sum(total * total) * kept, squares.shape)


def tokens_kernel(where, mine, out):
    for r in range(NX):
        owner = lax.rem(where[0] + r, NX)
        for g in range(NY * NZ):
            start = pl.multiple_of((owner * (NY * NZ) + g) * ROWS, ROWS)
            out[g, :, r * ROWS : (r + 1) * ROWS] = mine[:, pl.ds(start, ROWS)]


def near(x):
    return pltpu.with_memory_space_constraint(x, pltpu.VMEM)


SCALARS = pl.BlockSpec(memory_space=pltpu.SMEM)
GRANT = pltpu.CompilerParams(vmem_limit_bytes=8 * 2**20)
NEAR = pl.BlockSpec(memory_space=pltpu.VMEM)


def on_core(kernel, scalars, arrays, outs, scratch=()):
    return pl.pallas_call(
        kernel,
        in_specs=[SCALARS] * len(scalars) + [NEAR] * len(arrays),
        out_specs=[NEAR] * len(outs),
        out_shape=list(outs),
        scratch_shapes=scratch,
        compiler_params=GRANT,
    )(*scalars, *[near(a) for a in arrays])


def shift(x, axis, n, by):
    return lax.ppermute(x, axis, [(i, (i + by) % n) for i in range(n)])


def both(plus, minus, axis, n):
    return shift(plus, axis, n, 1), shift(minus, axis, n, -1)


def swap_side(x):
    return shift(x, "y_lo", NY, 1)


def first_terms(where, tails, acts):
    tokens = tails.shape[0]
    block = lambda x: lambda i, w: (
        0,
        x * (NY * NZ) + (1 - w[2]) * NZ + lax.rem(w[1] + NZ // 2, NZ),
    )
    whole = lambda *shape: pl.BlockSpec(shape, lambda i, w: (0, 0))
    shapes = (COLS, tokens), (2 * tokens, Z_WIDE)
    return pl.pallas_call(
        first_kernel,
        grid_spec=pltpu.PrefetchScalarGridSpec(
            num_scalar_prefetch=1,
            grid=(1,),
            in_specs=[whole(*tails.shape)]
            + [pl.BlockSpec((tokens, ROWS), block(x)) for x in range(NX)],
            out_specs=[whole(*shape) for shape in shapes],
            scratch_shapes=[pltpu.VMEM(tails.shape, bf16)],
        ),
        out_shape=[jax.ShapeDtypeStruct(shape, bf16) for shape in shapes],
        compiler_params=GRANT,
        name="work_first",
    )(where, tails, *([acts] * NX))


def sum_terms(where, tails, acts):
    tokens = acts.shape[0]
    two = lambda *shape: [pltpu.VMEM(shape, bf16)] * 2
    z_pairs, give = first_terms(where, tails, acts)
    wide = [2 * Z_WIDE] * (NZ // 2 - 1) + [Z_WIDE]
    gives = on_core(pack_kernel, [where], [acts], [pltpu.VMEM((tokens, w), bf16) for w in wide])
    joined, *parts = [swap_side(g) for g in [give, *gives]]

    sends = on_core(first_z_kernel, [where], [z_pairs, acts, joined], two(NX, HALF, ROWS))
    gots = both(*sends, "z", NZ)
    for s in range(1, NZ // 2):
        sends = on_core(
            functools.partial(later_z_kernel, s),
            [where],
            [z_pairs, acts, joined, parts[s - 1], *gots],
            two(NX, COLS, ROWS),
        )
        gots = both(*sends, "z", NZ)
    piece = lambda t: pltpu.VMEM((COLS, ROWS), t)
    (term,) = on_core(
        own_z_kernel, [where], [z_pairs, acts, joined, parts[-1]], [pltpu.VMEM((COLS, Z_WIDE), f32)]
    )
    own, *sends = on_core(
        last_z_kernel, [where], [term, *gots], [piece(f32)] + [piece(bf16)] * (NX - 1)
    )
    gots = [shift(send, "x", NX, r + 1) for r, send in enumerate(sends)]
    return own, gots


def local(
    activations, tail_grads, tail_slots, master, moment1, moment2, overflow, clip_on, next_inputs
):
    acts = activations[0]
    tails = tail_grads[0]
    tok_dev, width = acts.shape
    toks = next_inputs.shape[1]
    where = jnp.stack([lax.axis_index(a) for a in ("x", "z", "y_lo")]).astype(jnp.int32)
    where = jnp.concatenate([where, tail_slots[0, 0]])

    tokens = jax.ShapeDtypeStruct((NY * NZ, toks, NX * ROWS), bf16)
    (tokens,) = on_core(tokens_kernel, [where], [next_inputs[0]], [tokens])
    tokens = lax.all_to_all(tokens, YZ, 0, 0, tiled=True)

    own, gots = sum_terms(where, tails, acts)
    gradient, part_sq = on_core(
        functools.partial(gradient_kernel, 1.0 / (tok_dev * NX * NY * NZ)),
        [overflow],
        [own, *gots],
        [pltpu.VMEM((ROWS, COLS), f32), pltpu.VMEM((1, ROWS), f32)],
    )
    keep = (overflow[0, 0] == 0).astype(f32)
    for axes in (("y_hi", "core", "x"), YZ):
        part_sq = jnp.broadcast_to(part_sq[None], (4 * NX, 1, ROWS))
        part_sq = jnp.sum(lax.all_to_all(part_sq, axes, 0, 0, tiled=True), axis=0)
    sumsq = part_sq[0, 0]
    norm_value = jnp.sqrt(sumsq)
    factor = jnp.where(clip_on[0] == 1, 1.0 / jnp.maximum(norm_value, 1.0), 1.0)
    clipped = gradient * factor
    old_master = master[0]
    m_next = beta_one * moment1[0] + (1.0 - beta_one) * clipped
    v_next = beta_two * moment2[0] + (1.0 - beta_two) * (clipped * clipped)
    update = (
        m_next / correct_one / (jnp.sqrt(v_next / correct_two) + adam_eps) + decay_rate * old_master
    )
    updated = jnp.where(keep > 0.5, old_master - learn_rate * update, old_master)
    weights = updated.astype(bf16)

    along_x = jnp.concatenate(
        [weights] + [shift(weights, "x", NX, -r) for r in range(1, NX)], axis=0
    )
    partial = jnp.einsum("gtk,kc->gtc", tokens, along_x, preferred_element_type=f32).astype(bf16)
    parts = lax.all_to_all(partial, YZ, 0, 0, tiled=True)
    result = jnp.sum(parts.astype(f32), axis=0)
    next_out = (result * (1.0 / math.sqrt(width))).astype(bf16)
    return (updated[None], next_out[None])


def solution(mesh):
    finer = Mesh(mesh.devices.reshape(2, 2, NX, NY, NZ), EVERY)
    return jax.shard_map(
        local,
        mesh=finer,
        in_specs=(
            P(SECTION, DP, None),
            P(SECTION, DP, None),
            P(SECTION, DP, None),
            P(SECTION, DP, None),
            P(SECTION, DP, None),
            P(SECTION, DP, None),
            P(SECTION, DP),
            P(SECTION),
            P(SECTION, DP, None),
        ),
        out_specs=(P(SECTION, DP, None), P(SECTION, DP, None)),
        check_vma=False,
    )
```

```python
import functools
import math

import jax
import jax.numpy as jnp
from jax import lax
from jax.experimental import pallas as pl
from jax.experimental.pallas import tpu as pltpu
from jax.sharding import Mesh
from jax.sharding import PartitionSpec as P

DP = ("x", "y_lo", "z")
YZ = ("y_lo", "z")
SECTION = ("y_hi", "core")
EVERY = SECTION + DP

NX, NY, NZ = 4, 2, 8
TAILS = 4
COUNT = 4 * NX * NY * NZ


beta_one = 0.9
beta_two = 0.95
correct_one = 1.0 - 0.9**20
correct_two = 1.0 - 0.95**20
adam_eps = 1e-08
decay_rate = 0.1
learn_rate = 0.1

f32 = jnp.float32
bf16 = jnp.bfloat16

ROWS = 128
COLS = 512
HALF = COLS // 2
Z_WIDE = NX * ROWS


def column(x, y, z):
    return pl.multiple_of((x * (NY * NZ) + y * NZ + z) * ROWS, ROWS)


def side_columns(where, side, away, acts, turn=0):
    owner = lax.rem(where[1] + away, NZ)
    xs = [lax.rem(turn + k, NX) for k in range(NX)]
    return jnp.concatenate([acts[:, pl.ds(column(x, side, owner), ROWS)] for x in xs], axis=1)


def partner_pairs(joined):
    tail = joined[joined.shape[1] // 2 :, :]
    half = tail.shape[1] // 2
    return jnp.concatenate([tail[:, :half], tail[:, half:]], axis=0)


def z_terms(where, away, rows, pairs, acts, joined, part):
    own = jnp.dot(
        pairs[rows, :], side_columns(where, where[2], away, acts), preferred_element_type=f32
    )
    term = own + jnp.dot(partner_pairs(joined)[rows, :], part, preferred_element_type=f32)
    for k in range(NX):
        yield k, term[:, k * ROWS : (k + 1) * ROWS]


HALVES = slice(0, HALF), slice(HALF, COLS)


def first_kernel(where, tails, *refs):
    acts, (pairs, give, placed) = refs[:NX], refs[NX:]
    tail = tails.shape[0] // TAILS

    def place(t, carry):
        src = pl.ds(pl.multiple_of(t * tail, tail), tail)
        dst = pl.ds(pl.multiple_of(where[3 + t] * tail, tail), tail)
        placed[dst, :] = tails[src, :]
        return carry

    lax.fori_loop(0, TAILS, place, 0)
    tokens = tails.shape[0]
    value = placed[...].astype(f32).T.astype(bf16)
    pairs[...] = value
    for k in range(NX):
        give[:tokens, k * ROWS : (k + 1) * ROWS] = acts[k][...]
    give[tokens:, :tokens] = value[:HALF]
    give[tokens:, tokens:] = value[HALF:]


def pack_kernel(where, acts, *gives):
    for k, give in enumerate(gives):
        away = NZ // 2 - 1 - k
        for n, far in enumerate((away, NZ - away) if away else (0,)):
            give[:, n * Z_WIDE : (n + 1) * Z_WIDE] = side_columns(where, 1 - where[2], far, acts)


def first_z_kernel(where, pairs, acts, joined, out_p, out_m):
    part = joined[: acts.shape[0], :]
    for k, term in z_terms(where, NZ // 2, slice(0, COLS), pairs, acts, joined, part):
        out_p[k] = term[:HALF].astype(bf16)
        out_m[k] = term[HALF:].astype(bf16)


def later_z_kernel(s, half, ways, where, pairs, acts, joined, part, *refs):
    came, outs = dict(zip(ways, refs)), refs[len(ways) :]
    away = NZ // 2 - s
    for way, far in enumerate((away, NZ - away)):
        columns = slice(way * Z_WIDE, (way + 1) * Z_WIDE)
        for k, term in z_terms(where, far, HALVES[half], pairs, acts, joined, part[:, columns]):
            if way in came:
                term = term + came[way][k].astype(f32)
            outs[way][k] = term.astype(bf16)


def own_z_kernel(where, pairs, acts, joined, part, out):
    mine = jnp.dot(
        pairs[...], side_columns(where, where[2], 0, acts, where[0]), preferred_element_type=f32
    )
    xs = [lax.rem(where[0] + r, NX) for r in range(NX)]
    parts = [part[:, pl.ds(pl.multiple_of(x * ROWS, ROWS), ROWS)] for x in xs]
    out[...] = mine + jnp.dot(
        partner_pairs(joined), jnp.concatenate(parts, axis=1), preferred_element_type=f32
    )


def last_z_kernel(where, term, *refs):
    gots, own, sends = refs[:4], refs[4], refs[5:]
    for r in range(NX):
        x = lax.rem(where[0] + r, NX)
        for half, rows in enumerate(HALVES):
            up, down = gots[2 * half : 2 * half + 2]
            total = term[rows, r * ROWS : (r + 1) * ROWS] + up[x].astype(f32) + down[x].astype(f32)
            if r == 0:
                own[rows, :] = total
            else:
                sends[r - 1][rows, :] = total.astype(bf16)


def gradient_kernel(scale, overflow, own, *refs):
    gots, (grad, squares) = refs[: NX - 1], refs[NX - 1 :]
    total = own[...]
    for got in gots:
        total += got[...].astype(f32)
    total = total.T * scale
    grad[...] = total
    kept = jnp.where(overflow[0, 0] == 0, 1.0, 0.0)
    squares[...] = jnp.broadcast_to(jnp.sum(total * total) * kept, squares.shape)


def adam_kernel(overflow, clip_on, squares, grad, old_master, old_one, old_two, *refs):
    gots, states, (master, weights) = refs[: NX - 1], refs[NX - 1 : 2 * NX - 2], refs[2 * NX - 2 :]
    norm = jnp.sqrt(jnp.sum(squares[...], axis=0, keepdims=True))
    factor = jnp.where(clip_on[0] == 1, 1.0 / jnp.maximum(norm, 1.0), 1.0)
    own_keep = jnp.where(overflow[0, 0] == 0, 1.0, 0.0)
    for r in range(NX):
        for c in range(COLS // ROWS):
            lanes = slice(c * ROWS, (c + 1) * ROWS)
            if r == 0:
                old, one, two = (ref[:, lanes] for ref in (old_master, old_one, old_two))
                gradient = grad[:, lanes]
                keep = jnp.broadcast_to(own_keep, (1, ROWS))
            else:
                state = states[r - 1]
                old, one, two = (state[k * ROWS : (k + 1) * ROWS, lanes] for k in range(3))
                gradient = gots[r - 1][:, lanes].astype(f32)
                keep = state[3 * ROWS : 3 * ROWS + 1, lanes]
            clipped = gradient * factor
            m_next = beta_one * one + (1.0 - beta_one) * clipped
            v_next = beta_two * two + (1.0 - beta_two) * (clipped * clipped)
            update = (
                m_next / correct_one / (jnp.sqrt(v_next / correct_two) + adam_eps)
                + decay_rate * old
            )
            new = jnp.where(keep > 0.5, old - learn_rate * update, old)
            if r == 0:
                master[:, lanes] = new
            weights[r * ROWS : (r + 1) * ROWS, lanes] = new.astype(bf16)


def tokens_kernel(where, mine, out):
    for r in range(NX):
        owner = lax.rem(where[0] + r, NX)
        for g in range(NY * NZ):
            start = pl.multiple_of((owner * (NY * NZ) + g) * ROWS, ROWS)
            out[g, :, r * ROWS : (r + 1) * ROWS] = mine[:, pl.ds(start, ROWS)]


def near(x):
    return pltpu.with_memory_space_constraint(x, pltpu.VMEM)


def far(x):
    return pltpu.with_memory_space_constraint(x, pltpu.HBM)


SCALARS = pl.BlockSpec(memory_space=pltpu.SMEM)
GRANT = pltpu.CompilerParams(vmem_limit_bytes=8 * 2**20)
NEAR = pl.BlockSpec(memory_space=pltpu.VMEM)


def on_core(kernel, scalars, arrays, outs, scratch=(), place=near, grant=GRANT):
    return pl.pallas_call(
        kernel,
        in_specs=[SCALARS] * len(scalars) + [NEAR] * len(arrays),
        out_specs=[NEAR] * len(outs),
        out_shape=list(outs),
        scratch_shapes=scratch,
        compiler_params=grant,
    )(*scalars, *[place(a) for a in arrays])


def shift(x, axis, n, by):
    return lax.ppermute(x, axis, [(i, (i + by) % n) for i in range(n)])


def swap_side(x):
    return shift(x, "y_lo", NY, 1)


def first_terms(where, tails, acts):
    tokens = tails.shape[0]
    block = lambda x: lambda i, w: (
        0,
        x * (NY * NZ) + (1 - w[2]) * NZ + lax.rem(w[1] + NZ // 2, NZ),
    )
    whole = lambda *shape: pl.BlockSpec(shape, lambda i, w: (0, 0))
    shapes = (COLS, tokens), (2 * tokens, Z_WIDE)
    return pl.pallas_call(
        first_kernel,
        grid_spec=pltpu.PrefetchScalarGridSpec(
            num_scalar_prefetch=1,
            grid=(1,),
            in_specs=[whole(*tails.shape)]
            + [pl.BlockSpec((tokens, ROWS), block(x)) for x in range(NX)],
            out_specs=[whole(*shape) for shape in shapes],
            scratch_shapes=[pltpu.VMEM(tails.shape, bf16)],
        ),
        out_shape=[jax.ShapeDtypeStruct(shape, bf16) for shape in shapes],
        compiler_params=GRANT,
        name="work_first",
    )(where, far(tails), *([far(acts)] * NX))


def sum_terms(where, tails, acts):
    tokens = acts.shape[0]
    two = lambda *shape: [pltpu.VMEM(shape, bf16)] * 2
    z_pairs, give = first_terms(where, tails, acts)
    wide = [2 * Z_WIDE] * (NZ // 2 - 1) + [Z_WIDE]
    gives = on_core(pack_kernel, [where], [acts], [pltpu.VMEM((tokens, w), bf16) for w in wide])
    joined, *parts = [swap_side(g) for g in [give, *gives]]

    up, down = on_core(first_z_kernel, [where], [z_pairs, acts, joined], two(NX, HALF, ROWS))
    gots = {(0, 0): shift(up, "z", NZ, 1), (1, 1): shift(down, "z", NZ, -1)}
    for s in range(1, NZ // 2):
        came, gots = gots, {}
        for half in range(2):
            ways = [way for way in range(2) if (half, way) in came]
            up, down = on_core(
                functools.partial(later_z_kernel, s, half, ways),
                [where],
                [z_pairs, acts, joined, parts[s - 1], *[came[half, way] for way in ways]],
                two(NX, HALF, ROWS),
            )
            gots[half, 0] = shift(up, "z", NZ, 1)
            gots[half, 1] = shift(down, "z", NZ, -1)
    gots = [gots[half, way] for half in range(2) for way in range(2)]
    piece = lambda t: pltpu.VMEM((COLS, ROWS), t)
    (term,) = on_core(
        own_z_kernel, [where], [z_pairs, acts, joined, parts[-1]], [pltpu.VMEM((COLS, Z_WIDE), f32)]
    )
    own, *sends = on_core(
        last_z_kernel, [where], [term, *gots], [piece(f32)] + [piece(bf16)] * (NX - 1)
    )
    gots = [shift(send, "x", NX, r + 1) for r, send in enumerate(sends)]
    return own, gots


def local(
    activations, tail_grads, tail_slots, master, moment1, moment2, overflow, clip_on, next_inputs
):
    acts = activations[0]
    tails = tail_grads[0]
    tok_dev, width = acts.shape
    toks = next_inputs.shape[1]
    where = jnp.stack([lax.axis_index(a) for a in ("x", "z", "y_lo")]).astype(jnp.int32)
    where = jnp.concatenate([where, tail_slots[0, 0]])

    tokens = jax.ShapeDtypeStruct((NY * NZ, toks, NX * ROWS), bf16)
    (tokens,) = on_core(tokens_kernel, [where], [next_inputs[0]], [tokens])
    tokens = lax.all_to_all(tokens, YZ, 0, 0, tiled=True)

    keep = jnp.where(overflow[0, 0] == 0, 1.0, 0.0)
    state = [master[0], moment1[0], moment2[0], jnp.full((8, COLS), keep, f32)]
    state = jnp.concatenate(state, axis=0)
    states = [shift(state, "x", NX, -r) for r in range(1, NX)]

    own, gots = sum_terms(where, tails, acts)
    gradient, part_sq = on_core(
        functools.partial(gradient_kernel, 1.0 / (tok_dev * NX * NY * NZ)),
        [overflow],
        [own, *gots],
        [pltpu.VMEM((ROWS, COLS), f32), pltpu.VMEM((1, ROWS), f32)],
    )
    part_sq = jnp.broadcast_to(part_sq[None], (COUNT, 1, ROWS))
    squares = lax.all_to_all(part_sq, EVERY, 0, 0, tiled=True).reshape(COUNT, ROWS)
    gots = [shift(gradient.astype(bf16), "x", NX, -r) for r in range(1, NX)]
    updated, along_x = on_core(
        adam_kernel,
        [overflow, clip_on],
        [squares, gradient, master[0], moment1[0], moment2[0], *gots, *states],
        [
            jax.ShapeDtypeStruct((ROWS, COLS), f32),
            jax.ShapeDtypeStruct((NX * ROWS, COLS), bf16),
        ],
        place=lambda a: a,
        grant=pltpu.CompilerParams(vmem_limit_bytes=12 * 2**20),
    )
    partial = jnp.einsum("gtk,kc->gtc", tokens, along_x, preferred_element_type=f32).astype(bf16)
    parts = lax.all_to_all(partial, YZ, 0, 0, tiled=True)
    result = jnp.sum(parts.astype(f32), axis=0)
    next_out = (result * (1.0 / math.sqrt(width))).astype(bf16)
    return (updated[None], next_out[None])


def solution(mesh):
    finer = Mesh(mesh.devices.reshape(2, 2, NX, NY, NZ), EVERY)
    return jax.shard_map(
        local,
        mesh=finer,
        in_specs=(
            P(SECTION, DP, None),
            P(SECTION, DP, None),
            P(SECTION, DP, None),
            P(SECTION, DP, None),
            P(SECTION, DP, None),
            P(SECTION, DP, None),
            P(SECTION, DP),
            P(SECTION),
            P(SECTION, DP, None),
        ),
        out_specs=(P(SECTION, DP, None), P(SECTION, DP, None)),
        check_vma=False,
    )
```

```python
import functools
import math

import jax
import jax.numpy as jnp
from jax import lax
from jax.experimental import pallas as pl
from jax.experimental.pallas import tpu as pltpu
from jax.sharding import Mesh
from jax.sharding import PartitionSpec as P

DP = ("x", "y_lo", "z")
YZ = ("y_lo", "z")
SECTION = ("y_hi", "core")
EVERY = SECTION + DP

NX, NY, NZ = 4, 2, 8
TAILS = 4
COUNT = 4 * NX * NY * NZ


beta_one = 0.9
beta_two = 0.95
correct_one = 1.0 - 0.9**20
correct_two = 1.0 - 0.95**20
adam_eps = 1e-08
decay_rate = 0.1
learn_rate = 0.1

f32 = jnp.float32
bf16 = jnp.bfloat16

ROWS = 128
COLS = 512
HALF = COLS // 2
Z_WIDE = NX * ROWS


def column(x, y, z):
    return pl.multiple_of((x * (NY * NZ) + y * NZ + z) * ROWS, ROWS)


def side_columns(where, side, away, acts, turn=0):
    owner = lax.rem(where[1] + away, NZ)
    xs = [lax.rem(turn + k, NX) for k in range(NX)]
    return jnp.concatenate([acts[:, pl.ds(column(x, side, owner), ROWS)] for x in xs], axis=1)


def partner_pairs(joined):
    tail = joined[joined.shape[1] // 2 :, :]
    half = tail.shape[1] // 2
    return jnp.concatenate([tail[:, :half], tail[:, half:]], axis=0)


def z_terms(where, away, rows, pairs, acts, joined, part):
    own = jnp.dot(
        pairs[rows, :], side_columns(where, where[2], away, acts), preferred_element_type=f32
    )
    term = own + jnp.dot(partner_pairs(joined)[rows, :], part, preferred_element_type=f32)
    for k in range(NX):
        yield k, term[:, k * ROWS : (k + 1) * ROWS]


HALVES = slice(0, HALF), slice(HALF, COLS)


def first_kernel(where, tails, *refs):
    acts, (pairs, give, placed) = refs[:NX], refs[NX:]
    tail = tails.shape[0] // TAILS

    def place(t, carry):
        src = pl.ds(pl.multiple_of(t * tail, tail), tail)
        dst = pl.ds(pl.multiple_of(where[3 + t] * tail, tail), tail)
        placed[dst, :] = tails[src, :]
        return carry

    lax.fori_loop(0, TAILS, place, 0)
    tokens = tails.shape[0]
    value = placed[...].astype(f32).T.astype(bf16)
    pairs[...] = value
    for k in range(NX):
        give[:tokens, k * ROWS : (k + 1) * ROWS] = acts[k][...]
    give[tokens:, :tokens] = value[:HALF]
    give[tokens:, tokens:] = value[HALF:]


def pack_kernel(where, acts, *gives):
    for k, give in enumerate(gives):
        away = NZ // 2 - 1 - k
        for n, far in enumerate((away, NZ - away) if away else (0,)):
            give[:, n * Z_WIDE : (n + 1) * Z_WIDE] = side_columns(where, 1 - where[2], far, acts)


def first_z_kernel(where, pairs, acts, joined, out_p, out_m):
    part = joined[: acts.shape[0], :]
    for k, term in z_terms(where, NZ // 2, slice(0, COLS), pairs, acts, joined, part):
        out_p[k] = term[:HALF].astype(bf16)
        out_m[k] = term[HALF:].astype(bf16)


def later_z_kernel(s, half, ways, where, pairs, acts, joined, part, *refs):
    came, outs = dict(zip(ways, refs)), refs[len(ways) :]
    away = NZ // 2 - s
    for way, far in enumerate((away, NZ - away)):
        columns = slice(way * Z_WIDE, (way + 1) * Z_WIDE)
        for k, term in z_terms(where, far, HALVES[half], pairs, acts, joined, part[:, columns]):
            if way in came:
                term = term + came[way][k].astype(f32)
            outs[way][k] = term.astype(bf16)


def own_z_kernel(where, pairs, acts, joined, part, out):
    mine = jnp.dot(
        pairs[...], side_columns(where, where[2], 0, acts, where[0]), preferred_element_type=f32
    )
    xs = [lax.rem(where[0] + r, NX) for r in range(NX)]
    parts = [part[:, pl.ds(pl.multiple_of(x * ROWS, ROWS), ROWS)] for x in xs]
    out[...] = mine + jnp.dot(
        partner_pairs(joined), jnp.concatenate(parts, axis=1), preferred_element_type=f32
    )


def last_z_kernel(where, term, *refs):
    gots, own, sends = refs[:4], refs[4], refs[5:]
    for r in range(NX):
        x = lax.rem(where[0] + r, NX)
        for half, rows in enumerate(HALVES):
            up, down = gots[2 * half : 2 * half + 2]
            total = term[rows, r * ROWS : (r + 1) * ROWS] + up[x].astype(f32) + down[x].astype(f32)
            if r == 0:
                own[rows, :] = total
            else:
                sends[r - 1][rows, :] = total.astype(bf16)


def gradient_kernel(scale, overflow, own, *refs):
    gots, (grad, rounded, squares) = refs[: NX - 1], refs[NX - 1 :]
    total = own[...]
    for got in gots:
        total += got[...].astype(f32)
    total = total.T * scale
    grad[...] = total
    rounded[...] = total.astype(bf16)
    kept = jnp.where(overflow[0, 0] == 0, 1.0, 0.0)
    squares[...] = jnp.broadcast_to(jnp.sum(total * total) * kept, squares.shape)


def adam_kernel(overflow, clip_on, squares, grad, old_master, old_one, old_two, *refs):
    gots, states, (master, weights) = refs[: NX - 1], refs[NX - 1 : 2 * NX - 2], refs[2 * NX - 2 :]
    norm = jnp.sqrt(jnp.sum(squares[...], axis=0, keepdims=True))
    factor = jnp.where(clip_on[0] == 1, 1.0 / jnp.maximum(norm, 1.0), 1.0)
    own_keep = jnp.where(overflow[0, 0] == 0, 1.0, 0.0)
    for r in range(NX):
        for c in range(COLS // ROWS):
            lanes = slice(c * ROWS, (c + 1) * ROWS)
            if r == 0:
                old, one, two = (ref[:, lanes] for ref in (old_master, old_one, old_two))
                gradient = grad[:, lanes]
                keep = jnp.broadcast_to(own_keep, (1, ROWS))
            else:
                state = states[r - 1]
                old, one, two = (state[k * ROWS : (k + 1) * ROWS, lanes] for k in range(3))
                gradient = gots[r - 1][:, lanes].astype(f32)
                keep = state[3 * ROWS : 3 * ROWS + 1, lanes]
            clipped = gradient * factor
            m_next = beta_one * one + (1.0 - beta_one) * clipped
            v_next = beta_two * two + (1.0 - beta_two) * (clipped * clipped)
            update = (
                m_next / correct_one / (jnp.sqrt(v_next / correct_two) + adam_eps)
                + decay_rate * old
            )
            new = jnp.where(keep > 0.5, old - learn_rate * update, old)
            if r == 0:
                master[:, lanes] = new
            weights[r * ROWS : (r + 1) * ROWS, lanes] = new.astype(bf16)


def tokens_kernel(where, mine, out):
    for r in range(NX):
        owner = lax.rem(where[0] + r, NX)
        for g in range(NY * NZ):
            start = pl.multiple_of((owner * (NY * NZ) + g) * ROWS, ROWS)
            out[g, :, r * ROWS : (r + 1) * ROWS] = mine[:, pl.ds(start, ROWS)]


def near(x):
    return pltpu.with_memory_space_constraint(x, pltpu.VMEM)


def far(x):
    return pltpu.with_memory_space_constraint(x, pltpu.HBM)


SCALARS = pl.BlockSpec(memory_space=pltpu.SMEM)
GRANT = pltpu.CompilerParams(vmem_limit_bytes=8 * 2**20)
NEAR = pl.BlockSpec(memory_space=pltpu.VMEM)


def on_core(kernel, scalars, arrays, outs, scratch=(), place=near, grant=GRANT):
    return pl.pallas_call(
        kernel,
        in_specs=[SCALARS] * len(scalars) + [NEAR] * len(arrays),
        out_specs=[NEAR] * len(outs),
        out_shape=list(outs),
        scratch_shapes=scratch,
        compiler_params=grant,
    )(*scalars, *[place(a) for a in arrays])


def shift(x, axis, n, by):
    return lax.ppermute(x, axis, [(i, (i + by) % n) for i in range(n)])


def swap_side(x):
    return shift(x, "y_lo", NY, 1)


def first_terms(where, tails, acts):
    tokens = tails.shape[0]
    block = lambda x: lambda i, w: (
        0,
        x * (NY * NZ) + (1 - w[2]) * NZ + lax.rem(w[1] + NZ // 2, NZ),
    )
    whole = lambda *shape: pl.BlockSpec(shape, lambda i, w: (0, 0))
    shapes = (COLS, tokens), (2 * tokens, Z_WIDE)
    return pl.pallas_call(
        first_kernel,
        grid_spec=pltpu.PrefetchScalarGridSpec(
            num_scalar_prefetch=1,
            grid=(1,),
            in_specs=[whole(*tails.shape)]
            + [pl.BlockSpec((tokens, ROWS), block(x)) for x in range(NX)],
            out_specs=[whole(*shape) for shape in shapes],
            scratch_shapes=[pltpu.VMEM(tails.shape, bf16)],
        ),
        out_shape=[jax.ShapeDtypeStruct(shape, bf16) for shape in shapes],
        compiler_params=GRANT,
        name="work_first",
    )(where, far(tails), *([far(acts)] * NX))


def sum_terms(where, tails, acts):
    tokens = acts.shape[0]
    two = lambda *shape: [pltpu.VMEM(shape, bf16)] * 2
    loose = jax.ShapeDtypeStruct((NX, HALF, ROWS), bf16)
    z_pairs, give = first_terms(where, tails, acts)
    wide = [2 * Z_WIDE] * (NZ // 2 - 1) + [Z_WIDE]
    gives = on_core(pack_kernel, [where], [acts], [pltpu.VMEM((tokens, w), bf16) for w in wide])
    joined, *parts = [swap_side(g) for g in [give, *gives]]

    up, down = on_core(first_z_kernel, [where], [z_pairs, acts, joined], two(NX, HALF, ROWS))
    gots = {(0, 0): shift(up, "z", NZ, 1), (1, 1): shift(down, "z", NZ, -1)}
    for s in range(1, NZ // 2):
        came, gots = gots, {}
        for half in range(2):
            ways = [way for way in range(2) if (half, way) in came]
            up, down = on_core(
                functools.partial(later_z_kernel, s, half, ways),
                [where],
                [z_pairs, acts, joined, parts[s - 1], *[came[half, way] for way in ways]],
                two(NX, HALF, ROWS) if s + 1 < NZ // 2 else [loose] * 2,
            )
            gots[half, 0] = shift(up, "z", NZ, 1)
            gots[half, 1] = shift(down, "z", NZ, -1)
    gots = [gots[half, way] for half in range(2) for way in range(2)]
    piece = lambda t: pltpu.VMEM((COLS, ROWS), t)
    (term,) = on_core(
        own_z_kernel, [where], [z_pairs, acts, joined, parts[-1]], [pltpu.VMEM((COLS, Z_WIDE), f32)]
    )
    own, *sends = on_core(
        last_z_kernel, [where], [term, *gots], [piece(f32)] + [piece(bf16)] * (NX - 1)
    )
    gots = [shift(send, "x", NX, r + 1) for r, send in enumerate(sends)]
    return own, gots


def local(
    activations, tail_grads, tail_slots, master, moment1, moment2, overflow, clip_on, next_inputs
):
    acts = activations[0]
    tails = tail_grads[0]
    tok_dev, width = acts.shape
    toks = next_inputs.shape[1]
    where = jnp.stack([lax.axis_index(a) for a in ("x", "z", "y_lo")]).astype(jnp.int32)
    where = jnp.concatenate([where, tail_slots[0, 0]])

    tokens = jax.ShapeDtypeStruct((NY * NZ, toks, NX * ROWS), bf16)
    (tokens,) = on_core(tokens_kernel, [where], [next_inputs[0]], [tokens])
    tokens = lax.all_to_all(tokens, YZ, 0, 0, tiled=True)

    keep = jnp.where(overflow[0, 0] == 0, 1.0, 0.0)
    state = [master[0], moment1[0], moment2[0], jnp.full((8, COLS), keep, f32)]
    state = jnp.concatenate(state, axis=0)
    states = [shift(state, "x", NX, -r) for r in range(1, NX)]

    own, gots = sum_terms(where, tails, acts)
    gradient, rounded, part_sq = on_core(
        functools.partial(gradient_kernel, 1.0 / (tok_dev * NX * NY * NZ)),
        [overflow],
        [own, *gots],
        [
            pltpu.VMEM((ROWS, COLS), f32),
            jax.ShapeDtypeStruct((ROWS, COLS), bf16),
            jax.ShapeDtypeStruct((COUNT, ROWS), f32),
        ],
    )
    gots = [shift(rounded, "x", NX, -r) for r in range(1, NX)]
    part_sq = part_sq.reshape(COUNT, 1, ROWS)
    squares = lax.all_to_all(part_sq, EVERY, 0, 0, tiled=True).reshape(COUNT, ROWS)
    updated, along_x = on_core(
        adam_kernel,
        [overflow, clip_on],
        [squares, gradient, master[0], moment1[0], moment2[0], *gots, *states],
        [
            jax.ShapeDtypeStruct((ROWS, COLS), f32),
            jax.ShapeDtypeStruct((NX * ROWS, COLS), bf16),
        ],
        place=lambda a: a,
        grant=pltpu.CompilerParams(vmem_limit_bytes=12 * 2**20),
    )
    partial = jnp.einsum("gtk,kc->gtc", tokens, along_x, preferred_element_type=f32).astype(bf16)
    parts = lax.all_to_all(partial, YZ, 0, 0, tiled=True)
    result = jnp.sum(parts.astype(f32), axis=0)
    next_out = (result * (1.0 / math.sqrt(width))).astype(bf16)
    return (updated[None], next_out[None])


def solution(mesh):
    finer = Mesh(mesh.devices.reshape(2, 2, NX, NY, NZ), EVERY)
    return jax.shard_map(
        local,
        mesh=finer,
        in_specs=(
            P(SECTION, DP, None),
            P(SECTION, DP, None),
            P(SECTION, DP, None),
            P(SECTION, DP, None),
            P(SECTION, DP, None),
            P(SECTION, DP, None),
            P(SECTION, DP),
            P(SECTION),
            P(SECTION, DP, None),
        ),
        out_specs=(P(SECTION, DP, None), P(SECTION, DP, None)),
        check_vma=False,
    )
```
